512 devices in a mesh: morton: 32 (over z_lo, x, core), lane: 16 (over z_hi, y).
Axes of the slice: x: 4, y: 4, z: 16 (z_hi: 4, z_lo: 4; z = z_hi * 4 + z_lo), core: 2. Of those that a mesh axis runs over, the one named last changes fastest.
Arguments:
- multipoles: bfloat16 [32, 2048, 296], P('morton', 'lane'), may hold values from -6 to 6
- counts: int32 [32, 2048], P('morton', 'lane'), may hold values from 1 to 48
- sources: int32 [32, 2048, 48], P('morton', 'lane'), may hold values from 0 to 1151, as said below
- relpos: int32 [32, 2048, 48], P('morton', 'lane'), may hold values from 0 to 47, as said below
- operators: bfloat16 [48, 296, 296], P('lane'), may hold values from -0.375 to 0.375
- c2e: bfloat16 [296, 296], replicated, may hold values from -0.375 to 0.375
Outputs:
- local_density: float32 [32, 2048, 296], P('morton', 'lane')
The draws below stay inside these ranges and needn't reach their ends.
Inputs may be any that keep to these rules, and one draw needn't show every extreme that they name: `sources`: every live slot names a source box inside the grid of 32 x 16 devices' boxes. `relpos`: the ids of one box's slots are all different.
All inputs are finite; a program needn't handle non-finite values.
Results may differ from the reference program's by a relative error of at most 0.0029.
Values may be sent and summed in bfloat16 or wider, within the bound.
A program may use at most 64 MiB of HBM per device.

```python
import jax
import jax.numpy as jnp
from jax import lax

EQ = 296
BOX_DEV = 128
SEGS = 32
LANES = 16
REL = 48


def build_lists(key):
    keys = [jax.random.fold_in(key, 7100 + index) for index in range(8)]
    ndevice = SEGS * LANES
    nboxes = ndevice * BOX_DEV
    slot_ids = jnp.arange(REL, dtype=jnp.int32)
    scores = jax.random.randint(keys[0], (ndevice, REL), 0, 1 << 20) * REL + slot_ids[None, :]
    perm = jnp.argsort(scores, axis=1).astype(jnp.int32)
    active = jax.random.randint(keys[1], (ndevice,), 1, REL + 1)
    active = active.at[0].set(REL)
    owner = jnp.arange(nboxes, dtype=jnp.int32) // BOX_DEV
    box_active = active[owner]
    cnt = jax.random.randint(keys[2], (nboxes,), 0, 1 << 20) % box_active + 1
    cnt = cnt.at[0].set(REL)
    second = jax.random.randint(keys[3], (nboxes, REL), 0, 1 << 20) * REL + slot_ids[None, :]
    second = second + (slot_ids[None, :] >= box_active[:, None]).astype(jnp.int32) * (1 << 26)
    order = jnp.argsort(second, axis=1).astype(jnp.int32)
    rel = jnp.take_along_axis(perm[owner], order, axis=1)
    step_seg = jax.random.randint(keys[4], (nboxes, REL), -1, 2)
    step_lane = jax.random.randint(keys[5], (nboxes, REL), -1, 2)
    segment = (owner // LANES)[:, None]
    subrange = (owner % LANES)[:, None]
    seg_src = jnp.clip(segment + step_seg, 0, SEGS - 1)
    lane_src = jnp.clip(subrange + step_lane, 0, LANES - 1)
    neighbour = (seg_src - segment + 1) * 3 + (lane_src - subrange + 1)
    offset = jax.random.randint(keys[6], (nboxes, REL), 0, BOX_DEV)
    code = (neighbour * BOX_DEV + offset).astype(jnp.int32)
    return (cnt.astype(jnp.int32).reshape(SEGS, LANES * BOX_DEV), code.reshape(SEGS, LANES * BOX_DEV, REL), rel.astype(jnp.int32).reshape(SEGS, LANES * BOX_DEV, REL))


def draw_counts(key, part):
    return build_lists(key)[0]


def draw_sources(key, part):
    return build_lists(key)[1]


def draw_relpos(key, part):
    return build_lists(key)[2]


def level_of(key, shape, shards, smallest, top_value):
    factor_of = 1.0
    for dim, blocks in shards:
        heights = jax.random.uniform(jax.random.fold_in(jax.random.fold_in(key, 6), dim), (blocks,), jnp.float32, smallest / len(shards), top_value / len(shards))
        factor_of = factor_of * jnp.repeat(jnp.exp(heights), shape[dim] // blocks).reshape((-1,) + (1,) * (len(shape) - 1 - dim))
    return factor_of


def scatter_about(key, extent, scale, most, split=(), kind=jnp.bfloat16):
    level = level_of(key, extent, split, -0.22, 0.18) if split else 1.0
    array = jax.random.normal(key, extent, jnp.float32) * scale * level
    return jnp.minimum(jnp.maximum(array, -most), most).astype(kind)


def setup_inputs(seed: int = 0) -> dict:
    key_of = jax.random.split(jax.random.key(seed), 7)
    multipoles = scatter_about(key_of[0], (SEGS, LANES * BOX_DEV, EQ), 1.0, 6.0, ((0, 32), (1, 16)))
    counts = draw_counts(jax.random.fold_in(key_of[6], 71), 0)
    sources = draw_sources(jax.random.fold_in(key_of[6], 71), 0)
    relpos = draw_relpos(jax.random.fold_in(key_of[6], 71), 0)
    operators = scatter_about(key_of[4], (REL, EQ, EQ), EQ ** -0.5, 0.375, ((0, 16),))
    c2e = scatter_about(key_of[5], (EQ, EQ), EQ ** -0.5, 0.375)
    return {"multipoles": multipoles, "counts": counts, "sources": sources, "relpos": relpos, "operators": operators, "c2e": c2e}


def reference(multipoles, counts, sources, relpos, operators, c2e):
    flat = multipoles.reshape(SEGS * LANES * BOX_DEV, EQ)
    cnt = counts.reshape(SEGS * LANES, BOX_DEV)
    codes = sources.reshape(SEGS * LANES, BOX_DEV, REL)
    rel = relpos.reshape(SEGS * LANES, BOX_DEV, REL)
    slots = jnp.arange(REL, dtype=jnp.int32)
    devices = jnp.arange(SEGS * LANES, dtype=jnp.int32)

    def block(items):
        device, count_row, code_row, rel_row = items
        segment = device // LANES
        subrange = device % LANES
        neighbour = code_row // BOX_DEV
        offset = code_row % BOX_DEV
        seg_src = segment + neighbour // 3 - 1
        lane_src = subrange + neighbour % 3 - 1
        global_src = ((seg_src * LANES + lane_src) * BOX_DEV + offset).astype(jnp.int32)
        live = slots[None, :] < count_row[:, None]

        def step(index, total):
            hit = live & (rel_row == index)
            has = jnp.any(hit, axis=1)
            where_src = jnp.sum(jnp.where(hit, global_src, 0), axis=1).astype(jnp.int32)
            rows = jnp.where(has[:, None], flat[where_src], jnp.zeros((), flat.dtype))
            matrix = lax.dynamic_index_in_dim(operators, index, 0, keepdims=False)
            return total + jnp.dot(rows, matrix, preferred_element_type=jnp.float32)

        total = lax.fori_loop(0, REL, step, jnp.zeros((BOX_DEV, EQ), jnp.float32))
        check = total.astype(jnp.bfloat16)
        return jnp.dot(check, c2e, preferred_element_type=jnp.float32)

    result = lax.map(block, (devices, cnt, codes, rel))
    return result.reshape(SEGS, LANES * BOX_DEV, EQ)
```

```python
import jax
import jax.numpy as jnp
from jax import lax
from jax.experimental import pallas as pl
from jax.experimental.pallas import tpu as pltpu
from jax.sharding import Mesh
from jax.sharding import PartitionSpec as P

MESH = pl.DeviceIdType.MESH
F32 = jnp.float32
BF16 = jnp.bfloat16
MORTON = ("zl", "x", "core")
LANE = ("zh", "y")

RP = 320
RM = 304
PW = 896


def block_at(slot, a):
    return pl.ds(pl.multiple_of(128 * (3 * slot + a), 128), 128)


def kernel(mult, cnt, src, rel, ops, c2e, out, wide, pko, pk, tb, op, rem, rows, acc, ps, pr, send, recv):
    zl, x, c = lax.axis_index("zl"), lax.axis_index("x"), lax.axis_index("core")
    h, y = lax.axis_index("zh"), lax.axis_index("y")
    step = 1 - 2 * c
    m = (zl * 4 + x) * 2 + c

    def at_morton(k):
        k = lax.rem(k + 32, 32)
        return {"zl": k // 8, "x": lax.rem(k // 2, 4), "core": lax.rem(k, 2)}

    def at_y(d):
        return {"y": lax.rem(y + d + 4, 4)}

    def at_x(d):
        return {"x": lax.rem(x + d + 4, 4)}

    def at_h(d):
        return {"zh": lax.rem(h + d + 4, 4)}

    up, down = at_morton(m + 1), at_morton(m - 1)
    other = {"core": 1 - c}

    barrier = pltpu.get_barrier_semaphore()
    partners = [at_y(1), at_y(2), at_y(3), up, down, at_h(1), at_h(3), at_x(1), at_x(3)]
    partners += [{"zh": lax.rem(h + 3, 4), "y": 3}, {"zh": lax.rem(h + 1, 4), "y": 0}]
    for who in partners:
        pl.semaphore_signal(barrier, inc=1, device_id=who, device_id_type=MESH)

    def copy(n, src_ref, dst_ref, who, s=None):
        return pltpu.make_async_remote_copy(
            src_ref=src_ref, dst_ref=dst_ref, send_sem=send.at[n if s is None else s], recv_sem=recv.at[n],
            device_id=who, device_id_type=MESH,
        )

    wide[...] = jnp.zeros_like(wide)
    own = block_at(1 + y, 1)
    wide[0:128, 0:296] = mult[0].astype(F32)
    tb[:, own] = wide[0:128, :].T[0:RP].astype(BF16)
    for e in range(3):
        wide[0:296, 0:296] = ops[e].astype(F32)
        turned = wide[...].T
        op[0, :, 256 * e : 256 * e + 256] = turned[0:RP, 0:256].astype(BF16)
        last = turned[0:RP, 256:384]
        if e == 0:
            rest = last
        else:
            rest = rest + pltpu.roll(last, 40 * e, 1)
    op[0, :, 768:896] = rest.astype(BF16)
    wide[...] = jnp.zeros_like(wide)
    wide[0:128, 0:48] = rel[0].astype(F32)
    code = src[0]
    near = code >> 7
    a_of = (near * 11) >> 5
    b_of = near - 3 * a_of
    wide[0:128, 128:176] = ((b_of * 3 + a_of) * 128 + (code & 127)).astype(F32)
    relt = wide[0:128, 0:128].T[0:48]
    codet = wide[0:128, 128:256].T[0:48]
    live = lax.broadcasted_iota(jnp.int32, (48, 128), 0) < cnt[...]
    code1 = jnp.where(live, codet + 1.0, 0.0)
    pko[...] = jnp.zeros_like(pko)
    for yp in range(4):
        for s, off in enumerate((0, 3, 1, 2)):
            base = 12 * lax.rem(h + off, 4) + 3 * yp
            for e in range(3):
                want = (base + e).astype(F32)
                pko[yp, 3 * s + e : 3 * s + e + 1, :] = (
                    jnp.sum(jnp.where(relt == want, code1, 0.0), axis=0, keepdims=True) - 1.0
                )
    rem[...] = jnp.zeros_like(rem)

    is_end = ((y == 0) | (y == 3)).astype(jnp.int32)
    pl.semaphore_wait(barrier, 9 + 4 * is_end)

    xs = pl.ds(pl.multiple_of(80 * x, 16), 80)

    def xrows(d):
        return pl.ds(pl.multiple_of(80 * lax.rem(x + d + 4, 4), 16), 80)

    def erows(d):
        return pl.ds(pl.multiple_of(80 * lax.rem(y + d + 4, 4), 16), 80)

    started = []

    def go(cp):
        cp.start()
        started.append(cp)

    h_first = copy(0, op.at[0, xs], op.at[1 + c, xs], at_h(step))
    go(h_first)

    end0, end5 = block_at(0, 1), block_at(5, 1)

    @pl.when(y == 3)
    def _():
        for q in range(4):
            r = pl.ds(80 * q, 80)
            copy(1, tb.at[r, own], tb.at[r, end0], {"zh": lax.rem(h + 1, 4), "y": q}, s=60 + q).start()

    @pl.when(y == 0)
    def _():
        for q in range(4):
            r = pl.ds(80 * q, 80)
            copy(2, tb.at[r, own], tb.at[r, end5], {"zh": lax.rem(h + 3, 4), "y": q}, s=60 + q).start()

    def yblock(n, d, to):
        col = block_at(1 + lax.rem(y + d + 4, 4), 1)
        return copy(n, tb.at[:, col], tb.at[:, col], at_y(to))

    go(yblock(3, 0, 1))
    go(yblock(4, 0, -1))
    for d in (1, 2, 3):
        who = at_y(d)
        go(copy(4 + d, pko.at[who["y"]], pk.at[y], who))

    def mblock(n, slot, up_or_down):
        if up_or_down > 0:
            return copy(n, tb.at[:, block_at(slot, 1)], tb.at[:, block_at(slot, 0)], up)
        return copy(n, tb.at[:, block_at(slot, 1)], tb.at[:, block_at(slot, 2)], down)

    def mpair(n, slot):
        go(mblock(n, slot, 1))
        go(mblock(n + 1, slot, -1))

    def mwait(n, slot):
        copy(n, tb.at[:, block_at(slot, 0)], tb.at[:, block_at(slot, 0)], up).wait_recv()
        copy(n + 1, tb.at[:, block_at(slot, 2)], tb.at[:, block_at(slot, 2)], up).wait_recv()

    mpair(10, 1 + y)
    ybehind = lax.rem(y - step + 4, 4)
    yahead = lax.rem(y + step + 4, 4)
    yfar = lax.rem(y + 2, 4)

    def ywait(n, yy):
        col = block_at(1 + yy, 1)
        copy(n, tb.at[:, col], tb.at[:, col], at_y(1)).wait_recv()

    def ywait_two():
        ywait(3, lax.rem(y + 3, 4))
        ywait(4, lax.rem(y + 1, 4))

    ywait_two()
    colb = block_at(1 + ybehind, 1)
    go(copy(8, tb.at[:, colb], tb.at[:, colb], at_y(step)))
    mpair(12, 1 + ybehind)
    mpair(14, 1 + yahead)
    ywait(8, yfar)
    mpair(16, 1 + yfar)

    eh = erows(0)
    copy(1, tb.at[eh, end0], tb.at[eh, end0], at_y(1)).wait_recv()
    copy(2, tb.at[eh, end5], tb.at[eh, end5], at_y(1)).wait_recv()
    for d in (1, 2, 3):
        go(copy(17 + d, tb.at[eh, end0], tb.at[eh, end0], at_y(d)))
        go(copy(20 + d, tb.at[eh, end5], tb.at[eh, end5], at_y(d)))
    for d in (1, 2, 3):
        e = erows(-d)
        copy(17 + d, tb.at[e, end0], tb.at[e, end0], at_y(d)).wait_recv()
        copy(20 + d, tb.at[e, end5], tb.at[e, end5], at_y(d)).wait_recv()
    mpair(24, 0)
    mpair(26, 5)

    def opslice(slot, r, lanes):
        return op.at[slot, r, lanes] if lanes is not None else op.at[slot, r]

    def op_wait(n, slot, r, lanes):
        ref = opslice(slot, r, lanes)
        copy(n, ref, ref, other).wait_recv()

    def op_send(n, slot, r, lanes, who):
        ref = opslice(slot, r, lanes)
        return copy(n, ref, ref, who)

    mine = 1 + c
    op_wait(0, mine, xs, None)
    LO, HI = pl.ds(0, 512), pl.ds(512, 384)

    @pl.when(c == 0)
    def _():
        copy(30, op.at[1, xs, LO], op.at[3, xs, LO], at_h(1)).start()

    @pl.when(c == 1)
    def _():
        copy(30, op.at[2, xs, HI], op.at[3, xs, HI], at_h(3)).start()

    def xstage(n, slot, lanes):
        op_send(n, slot, xs, lanes, at_x(1)).start()
        op_send(n + 1, slot, xs, lanes, at_x(-1)).start()
        op_send(n + 3, slot, xs, lanes, other).start()
        op_wait(n, slot, xrows(-1), lanes)
        op_wait(n + 1, slot, xrows(1), lanes)
        op_send(n + 2, slot, xrows(-step), lanes, at_x(step)).start()
        op_send(n + 4, slot, xrows(-1), lanes, other).start()
        op_send(n + 5, slot, xrows(1), lanes, other).start()
        op_wait(n + 2, slot, xrows(2), lanes)
        op_send(n + 6, slot, xrows(2), lanes, other).start()

    def xsent(n, slot, lanes):
        for k, d in ((0, 0), (1, 0), (2, 0), (3, 0), (4, -1), (5, 1), (6, 2)):
            op_send(n + k, slot, xrows(d), lanes, other).wait_send()

    def cwait(n, slot, lanes):
        for k, d in ((3, 0), (4, -1), (5, 1), (6, 2)):
            op_wait(n + k, slot, xrows(d), lanes)

    xstage(31, mine, None)

    @pl.when(c == 0)
    def _():
        op_wait(30, 3, xs, LO)
        xstage(38, 3, LO)
        xsent(38, 3, LO)
        op_send(30, 3, xs, LO, other).wait_send()

    @pl.when(c == 1)
    def _():
        op_wait(30, 3, xs, HI)
        xstage(38, 3, HI)
        xsent(38, 3, HI)
        op_send(30, 3, xs, HI, other).wait_send()

    pk[y] = pko[y]
    for d in (1, 2, 3):
        copy(4 + d, pko.at[0], pk.at[lax.rem(y - d + 4, 4)], at_y(d)).wait_recv()
    mwait(10, 1 + y)
    mwait(12, 1 + ybehind)
    mwait(14, 1 + yahead)
    mwait(16, 1 + yfar)
    mwait(24, 0)
    mwait(26, 5)

    place = lax.broadcasted_iota(jnp.int32, (1152, 128), 0).astype(F32)

    def gather(lam, _):
        cols = pl.ds(pl.multiple_of(384 * lam, 128), 1152)
        to = pl.ds(pl.multiple_of(128 * lam, 128), 128)

        def pair(s, _):
            for e in range(3):
                want = pk[lam, pl.ds(3 * s + e, 1), :]
                hot = jnp.where(place == want, 1.0, 0.0).astype(BF16)
                got = jnp.dot(tb[0:RM, cols], hot, preferred_element_type=F32)
                rows[s, 256 * e : 256 * e + 256, to] = got[0:256].astype(BF16)
                rem[s, 40 * e : 40 * e + 40, to] = got[256:296]
            return 0

        lax.fori_loop(0, 4, pair, 0)
        return 0

    lax.fori_loop(0, 4, gather, 0)

    @pl.when(c == 0)
    def _():
        cwait(31, 2, None)
        cwait(38, 3, HI)

    @pl.when(c == 1)
    def _():
        cwait(31, 1, None)
        cwait(38, 3, LO)

    xsent(31, mine, None)
    for s in range(4):
        rows[s, 768:896, :] = rem[s].astype(BF16)
        part = jnp.dot(op[s, 0:RM, :], rows[s], preferred_element_type=F32)
        if s == 0:
            acc[...] = part
        else:
            acc[...] += part

    for lam in range(4):
        ps[lam] = acc[:, 128 * lam : 128 * lam + 128].astype(BF16)
    for d in (1, 2, 3):
        who = at_y(d)
        go(copy(45 + d, ps.at[who["y"]], pr.at[d - 1], who))
    total = acc[:, pl.ds(pl.multiple_of(128 * y, 128), 128)]
    for d in (1, 2, 3):
        copy(45 + d, ps.at[0], pr.at[d - 1], at_y(d)).wait_recv()
    for d in range(3):
        total = total + pr[d].astype(F32)
    wide[0:RM, 0:128] = total
    wide[RM:384, 0:128] = jnp.zeros((384 - RM, 128), F32)
    check = wide[:, 0:128].T
    high = check.astype(BF16)
    low = (check - high.astype(F32)).astype(BF16)
    out[0] = jnp.dot(high[:, 0:296], c2e[...], preferred_element_type=F32) + jnp.dot(
        low[:, 0:296], c2e[...], preferred_element_type=F32
    )

    for cp in started:
        cp.wait_send()

    @pl.when(y == 3)
    def _():
        for q in range(4):
            r = pl.ds(80 * q, 80)
            copy(1, tb.at[r, own], tb.at[r, end0], at_h(1), s=60 + q).wait_send()

    @pl.when(y == 0)
    def _():
        for q in range(4):
            r = pl.ds(80 * q, 80)
            copy(2, tb.at[r, own], tb.at[r, end5], at_h(1), s=60 + q).wait_send()


def per_device(multipoles, counts, sources, relpos, operators, c2e):
    vmem = pl.BlockSpec(memory_space=pltpu.VMEM)
    return pl.pallas_call(
        kernel,
        out_shape=jax.ShapeDtypeStruct((1, 128, 296), F32),
        in_specs=[vmem] * 6,
        out_specs=vmem,
        scratch_shapes=[
            pltpu.VMEM((384, 384), F32),
            pltpu.VMEM((4, 16, 128), F32),
            pltpu.VMEM((4, 16, 128), F32),
            pltpu.VMEM((RP, 18 * 128), BF16),
            pltpu.VMEM((4, RP, PW), BF16),
            pltpu.VMEM((4, 128, 512), F32),
            pltpu.VMEM((4, PW, 512), BF16),
            pltpu.VMEM((RM, 512), F32),
            pltpu.VMEM((4, RM, 128), BF16),
            pltpu.VMEM((3, RM, 128), BF16),
            pltpu.SemaphoreType.DMA((64,)),
            pltpu.SemaphoreType.DMA((64,)),
        ],
        compiler_params=pltpu.CompilerParams(collective_id=0, has_side_effects=True, vmem_limit_bytes=48 * 1024 * 1024),
    )(multipoles, counts, sources, relpos, operators, c2e)


def solution(mesh):
    finer = Mesh(mesh.devices.reshape(4, 4, 2, 4, 4), MORTON + LANE)
    in_specs = (
        P(MORTON, LANE, None),
        P(MORTON, LANE),
        P(MORTON, LANE, None),
        P(MORTON, LANE, None),
        P(LANE, None, None),
        P(),
    )
    return jax.shard_map(
        per_device, mesh=finer, in_specs=in_specs, out_specs=P(MORTON, LANE, None), check_vma=False
    )
```
